512 devices in a mesh: rows: 64 (over x, z, core), cols: 8 (over y).
Axes of the slice: x: 4, y: 8, z: 8, core: 2. Of those that a mesh axis runs over, the one named last changes fastest.
Arguments:
- columns: float32 [65536, 3072], P('rows', 'cols'), may hold values from -4 to 4
- row_bases: float32 [4, 65536, 128], P(None, 'rows'), may hold values from -6 to 6
- order: int32 [64, 1024], P('rows'), may hold values from 0 to 1023, each once within a row
Outputs:
- solved: float32 [65536, 2560], P('rows', 'cols')
The draws below stay inside these ranges and needn't reach their ends.
Inputs may be any that keep to these rules, and one draw needn't show every extreme that they name: Each row of order is a permutation of 0 to 1023.
All inputs are finite; a program needn't handle non-finite values.
Results may differ from the reference program's by a relative error of at most 0.01.
Values sent between devices are 32-bit elements; how exact they have to be, the bound alone decides.
No kernel may reach another device: no remote copies, remote signals or barrier semaphores. Data moves between devices by JAX's collectives and lax.ppermute only.
A program may use at most 64 MiB of HBM per device.

```python
import math
import jax
import jax.numpy as jnp
from jax import lax

R = 128
LEVELS = 4
ROWS_DEV = 1024
TGT_DEV = 320
N = 65536
COLS = 3072
N_ROWS = 64
N_COLS = 8


def draw_columns(key, part):
    base = jax.random.fold_in(key, 23)
    noise_key = jax.random.fold_in(base, 0)
    noise = jax.random.normal(noise_key, (N, COLS), jnp.float32)
    return jnp.clip(noise, -4.0, 4.0)


def draw_row_bases(key, part):
    base = jax.random.fold_in(key, 11)
    noise_key, scale_key = jax.random.split(base)
    most_children = 2 ** LEVELS
    low_end, high_end = (1.35, 1.55)
    noise = jax.random.normal(noise_key, (LEVELS, N, R), jnp.float32)
    logs = jax.random.uniform(scale_key, (LEVELS, most_children), jnp.float32, math.log(low_end), math.log(high_end))
    steps = jnp.arange(LEVELS, dtype=jnp.float32)
    damping = jnp.where(steps < 0.5, 1.0, 0.3 * 0.87 ** jnp.maximum(steps - 1.0, 0.0))
    factors = jnp.exp(logs) * damping[:, None]
    points = jnp.arange(N, dtype=jnp.int32)
    row_scales = jnp.stack([factors[level][points // (N // 2 ** (LEVELS - level))] for level in range(LEVELS)])
    return jnp.clip(noise * row_scales[:, :, None], -6.0, 6.0)


def setup_inputs(seed: int = 0) -> dict:
    streams_of = jax.random.split(jax.random.key(seed), 4)
    columns = draw_columns(jax.random.fold_in(streams_of[3], 71), 0)
    row_bases = draw_row_bases(jax.random.fold_in(streams_of[3], 71), 0)
    order = jax.vmap(lambda own: jax.random.permutation(own, ROWS_DEV))(jax.random.split(streams_of[2], N_ROWS)).reshape((N_ROWS, ROWS_DEV)).astype(jnp.int32)
    return {"columns": columns, "row_bases": row_bases, "order": order}


HIGH = lax.Precision.HIGHEST

def solve_system(coupled, right_side):
    gram = jnp.einsum('...ki,...kj->...ij', coupled, coupled, precision=HIGH)
    factor = jnp.linalg.cholesky(gram)
    projected = jnp.einsum('...ki,...kq->...iq', coupled, right_side, precision=HIGH)
    middle = lax.linalg.triangular_solve(factor, projected, left_side=True, lower=True)
    return lax.linalg.triangular_solve(factor, middle, left_side=True, lower=True, transpose_a=True)

def reference(columns, row_bases, order):
    width_block = R // N_COLS
    block_cols = TGT_DEV + LEVELS * width_block
    total = ROWS_DEV * N_ROWS
    offsets = (jnp.arange(N_ROWS, dtype=jnp.int32) * ROWS_DEV)[:, None]
    places = (offsets + order.astype(jnp.int32)).reshape(-1).astype(jnp.int32)
    tree = jnp.take(columns, places, axis=0).reshape(total, N_COLS, block_cols)
    for level in range(LEVELS):
        start = TGT_DEV + (LEVELS - 1 - level) * width_block
        nodes = 2 ** (LEVELS - level - 1)
        child = total // (2 * nodes)
        scale = 0.55 / math.sqrt(R * child)
        upper = tree[:, :, :start].reshape(nodes, 2, child, N_COLS * start)
        basis = tree[:, :, start:start + width_block].reshape(nodes, 2, child, R)
        feats = row_bases[level].reshape(nodes, 2, child, R)
        proj = scale * jnp.einsum('nscr,nscq->nsrq', feats, upper, precision=HIGH)
        couple = scale * jnp.einsum('nscr,nscq->nsrq', feats, basis, precision=HIGH)
        ident = jnp.broadcast_to(jnp.eye(R, dtype=couple.dtype), (nodes, R, R))
        top = jnp.concatenate([ident, couple[:, 1]], axis=-1)
        bottom = jnp.concatenate([couple[:, 0], ident], axis=-1)
        system = jnp.concatenate([top, bottom], axis=-2)
        right_side = jnp.concatenate([proj[:, 1], proj[:, 0]], axis=-2)
        coeffs = solve_system(system, right_side).reshape(nodes, 2, R, N_COLS * start)
        update = jnp.einsum('nscr,nsrq->nscq', basis, coeffs, precision=HIGH)
        upper = (upper - update).reshape(total, N_COLS, start)
        tree = jnp.concatenate([upper, tree[:, :, start:]], axis=-1)
    targets = tree[:, :, :TGT_DEV].reshape(total, N_COLS * TGT_DEV)
    return jnp.zeros_like(targets).at[places].set(targets)
```

```python
import functools
import math

import jax
import jax.numpy as jnp
from jax import lax
from jax.experimental import pallas as pl
from jax.experimental.pallas import tpu as pltpu
from jax.sharding import Mesh, PartitionSpec as P

R = 128
LEVELS = 4
WB = 16
GROUPS = 8
ROW_AXES = ("x2", "x1", "z4", "z2", "z1", "core")
HIGH = lax.Precision.HIGHEST
F32 = jnp.float32
BF16 = jnp.bfloat16


def halves(x):
    hi = x.astype(BF16)
    return hi, (x - hi.astype(F32)).astype(BF16)


def mm(a, b):
    dot = functools.partial(jnp.dot, preferred_element_type=F32)
    return dot(a[0], b[0]) + (dot(a[0], b[1]) + dot(a[1], b[0]))


def exact(a, b, dims):
    return lax.dot_general(a, b, ((dims[0], dims[1]), ((), ())), precision=HIGH, preferred_element_type=F32)


def spd_inverse(g):
    lane = lax.broadcasted_iota(jnp.int32, (8, R), 1)
    sub = lax.broadcasted_iota(jnp.int32, (8, R), 0)
    n = R // 8
    tiles = [g[8 * i : 8 * i + 8, :] for i in range(n)]
    full = lambda v: jnp.broadcast_to(v, (8, R))
    for k in range(0, R, 4):
        p, s = k // 8, k % 8
        cols = [[full(tiles[i][:, k + j : k + j + 1]) for i in range(n)] for j in range(4)]
        panel = (lane >= k) & (lane < k + 4)
        rows = [
            jnp.where(lane == k + j, 1.0, jnp.where(panel, 0.0, full(tiles[p][s + j : s + j + 1, :])))
            for j in range(4)
        ]
        d = [[full(cols[j][p][s + i : s + i + 1, :]) for j in range(4)] for i in range(4)]
        r = 1.0 / (d[0][0] * d[1][1] - d[0][1] * d[1][0])
        p00, p01, p10, p11 = d[1][1] * r, -d[0][1] * r, -d[1][0] * r, d[0][0] * r
        e = [
            [p00 * d[0][2] + p01 * d[1][2], p00 * d[0][3] + p01 * d[1][3]],
            [p10 * d[0][2] + p11 * d[1][2], p10 * d[0][3] + p11 * d[1][3]],
        ]
        c = [
            [d[2 + i][2 + j] - (d[2 + i][0] * e[0][j] + d[2 + i][1] * e[1][j]) for j in range(2)]
            for i in range(2)
        ]
        q = 1.0 / (c[0][0] * c[1][1] - c[0][1] * c[1][0])
        t0 = p00 * rows[0] + p01 * rows[1]
        t1 = p10 * rows[0] + p11 * rows[1]
        u0 = rows[2] - (d[2][0] * t0 + d[2][1] * t1)
        u1 = rows[3] - (d[3][0] * t0 + d[3][1] * t1)
        v0 = (c[1][1] * u0 - c[0][1] * u1) * q
        v1 = (c[0][0] * u1 - c[1][0] * u0) * q
        new = [t0 - (e[0][0] * v0 + e[0][1] * v1), t1 - (e[1][0] * v0 + e[1][1] * v1), v0, v1]
        for i in range(n):
            a = jnp.where(panel, 0.0, tiles[i])
            for j in range(4):
                a = a - cols[j][i] * new[j]
            if i == p:
                for j in range(4):
                    a = jnp.where(sub == s + j, new[j], a)
            tiles[i] = a
    return jnp.concatenate(tiles, axis=0)


def pair_inverse(own, sib):
    i = lax.broadcasted_iota(jnp.int32, (R, R), 0)
    j = lax.broadcasted_iota(jnp.int32, (R, R), 1)
    m = jnp.where(i == j, 1.0, 0.0) - exact(own, sib, ((1,), (0,)))
    return exact(spd_inverse(exact(m, m, ((0,), (0,)))), m, ((1,), (1,)))


def coefficients(p_own, p_sib, a_own, a_sib, inv):
    c_own = mm(halves(p_sib - mm(halves(p_own), a_sib)), inv)
    c_own_h = halves(c_own)
    c_sib_h = halves(p_own - mm(c_own_h, a_own))
    return c_own, c_own_h, c_sib_h


def project_kernel(order_ref, x_ref, v_ref, scale, ht_ref, hw_ref):
    rows, width = x_ref.shape
    tgt = width - LEVELS * WB
    xt = x_ref[...].T
    hi, lo = halves(xt)
    at = lax.broadcasted_iota(jnp.int32, (rows, rows), 0)
    onehot = jnp.where(at == order_ref[...], 1.0, 0.0).astype(BF16)
    hi = jnp.dot(hi, onehot, preferred_element_type=F32).astype(BF16)
    lo = jnp.dot(lo, onehot, preferred_element_type=F32).astype(BF16)
    for level in range(LEVELS):
        h = mm((hi, lo), halves(v_ref[level])) * scale[level]
        ht_ref[:, R * level : R * level + R] = h[:tgt]
        for m in range(LEVELS):
            at_m = tgt + (LEVELS - 1 - m) * WB
            hw_ref[m * WB : m * WB + WB, R * level : R * level + R] = h[at_m : at_m + WB]


def block(ref, side, row, lanes):
    part = ref[side, :, row : row + WB, lanes]
    return part.reshape(GROUPS * WB, part.shape[-1])


def first_kernel(side_ref, crit_ref, inv_ref, next_ref):
    own, sib = side_ref[0], 1 - side_ref[0]
    lo, hi = slice(0, R), slice(R, 2 * R)
    a_own, a_sib = block(crit_ref, own, 0, lo), block(crit_ref, sib, 0, lo)
    inv = pair_inverse(a_own, a_sib)
    inv_ref[...] = inv
    _, c_own, c_sib = coefficients(
        block(crit_ref, own, WB, lo), block(crit_ref, sib, WB, lo), halves(a_own), halves(a_sib), halves(inv)
    )
    next_ref[...] = (block(crit_ref, own, WB, hi) + block(crit_ref, sib, WB, hi)) - (
        mm(c_own, halves(block(crit_ref, own, 0, hi))) + mm(c_sib, halves(block(crit_ref, sib, 0, hi)))
    )


def first_update_kernel(side_ref, inv_ref, crit_ref, rest_ref, t_own_ref, t_sib_ref, next_ref, c_ref):
    own, sib = side_ref[0], 1 - side_ref[0]
    lo, hi, more, deep = slice(0, R), slice(R, 2 * R), slice(0, 2 * R), slice(2 * R, 6 * R)

    def whole(side, t_ref):
        top = jnp.concatenate([block(crit_ref, side, 0, slice(0, 2 * R)), block(rest_ref, side, 0, more)], axis=1)
        second = jnp.concatenate([block(crit_ref, side, WB, slice(0, 2 * R)), block(rest_ref, side, WB, more)], axis=1)
        third, fourth = block(rest_ref, side, 0, deep), block(rest_ref, side, WB, deep)
        return top, jnp.concatenate([second, third, fourth, t_ref[...]], axis=0)

    top_own, low_own = whole(own, t_own_ref)
    top_sib, low_sib = whole(sib, t_sib_ref)
    update(top_own, low_own, top_sib, low_sib, inv_ref[...], next_ref, c_ref)


def update(top_own, low_own, top_sib, low_sib, inv, next_ref, c_ref):
    a_own, a_sib = halves(top_own[:, :R]), halves(top_sib[:, :R])
    c, c_own, c_sib = coefficients(low_own[:, :R], low_sib[:, :R], a_own, a_sib, halves(inv))
    c_ref[...] = c
    if next_ref is not None:
        next_ref[...] = (low_own[:, R:] + low_sib[:, R:]) - (
            mm(c_own, halves(top_own[:, R:])) + mm(c_sib, halves(top_sib[:, R:]))
        )


def inverse_kernel(own_ref, sib_ref, inv_ref):
    inv_ref[...] = pair_inverse(own_ref[...], sib_ref[...])


def update_kernel(inv_ref, own_ref, sib_ref, next_ref, c_ref):
    update(own_ref[:R], own_ref[R:], sib_ref[:R], sib_ref[R:], inv_ref[...], next_ref, c_ref)


def total_kernel(a_own_ref, a_sib_ref, t_own_ref, t_sib_ref, c0_ref, c1_ref, c2_ref, k_ref):
    a_own, a_sib = a_own_ref[...], a_sib_ref[...]
    inv = pair_inverse(a_own, a_sib)
    k3, k3h, _ = coefficients(t_own_ref[...], t_sib_ref[...], halves(a_own), halves(a_sib), halves(inv))
    w = lambda ref, m: halves(ref[m * R : m * R + R])
    k2 = c2_ref[R:] - mm(k3h, w(c2_ref, 0))
    k2h = halves(k2)
    k1 = c1_ref[2 * R :] - (mm(k2h, w(c1_ref, 0)) + mm(k3h, w(c1_ref, 1)))
    k1h = halves(k1)
    k0 = c0_ref[3 * R :] - (mm(k1h, w(c0_ref, 0)) + mm(k2h, w(c0_ref, 1)) + mm(k3h, w(c0_ref, 2)))
    for level, k in enumerate((k0, k1, k2, k3)):
        k_ref[:, R * level : R * level + R] = k


def final_kernel(core_ref, x_ref, w_ref, k_own_ref, k_sib_ref, out_ref):
    tgt = out_ref.shape[1]
    half = tgt // 2
    core = core_ref[0]
    rows = x_ref.shape[0]
    own, sib = k_own_ref[...], k_sib_ref[...]
    k = halves(jnp.concatenate([jnp.where(core == 0, own, sib), jnp.where(core == 0, sib, own)], axis=0))
    total = jnp.zeros((tgt, rows), F32)
    for level in range(LEVELS):
        at = (LEVELS - 1 - level) * WB
        w = halves(w_ref[:, at : at + WB, :].reshape(GROUPS * WB, rows))
        part = slice(R * level, R * level + R)
        total = total + mm((k[0][:, part], k[1][:, part]), w)
    out_ref[...] = x_ref[:, :tgt] - total.T


def call(kernel, outs, name, scalar=False):
    shapes = [jax.ShapeDtypeStruct(s, F32) for s in outs]
    single = len(shapes) == 1
    vmem = pl.BlockSpec(memory_space=pltpu.VMEM)

    def run(*args):
        specs = [vmem] * len(args)
        if scalar:
            specs[0] = pl.BlockSpec(memory_space=pltpu.SMEM)
        return pl.pallas_call(
            kernel,
            out_shape=shapes[0] if single else shapes,
            in_specs=specs,
            out_specs=vmem if single else [vmem] * len(shapes),
            name=name,
            compiler_params=pltpu.CompilerParams(vmem_limit_bytes=56 * 2**20),
        )(*args)

    return run


def swap(v, axis):
    return lax.ppermute(v, axis, [(0, 1), (1, 0)])


def gather(v, axes):
    n = lax.axis_size(axes)
    return lax.all_to_all(jnp.broadcast_to(v[None], (n, *v.shape)), axes, 0, 0, tiled=True)


def after(v, token):
    return lax.optimization_barrier((v, token))[0]


def on_device(columns, row_bases, order):
    rows, width = columns.shape
    tgt = width - LEVELS * WB
    half = tgt // 2
    scale = [0.55 / math.sqrt(R * rows * (4 << level)) for level in range(LEVELS)]
    core = lax.axis_index("core")
    side = lax.axis_index("z2").astype(jnp.int32)[None]

    def project(order_ref, x_ref, v_ref, ht_ref, hw_ref):
        project_kernel(order_ref, x_ref, v_ref, scale, ht_ref, hw_ref)

    ht, hw = call(project, [(tgt, LEVELS * R), (LEVELS * WB, LEVELS * R)], "project")(order, columns, row_bases)

    hw = hw + swap(hw, "core")
    hw = hw + swap(hw, "z1")
    crit = gather(hw[: 2 * WB, : 2 * R], ("z2", "cols")).reshape(2, GROUPS, 2 * WB, 2 * R)
    keep = lax.dynamic_slice_in_dim(ht, core * half, half, 0)
    give = lax.dynamic_slice_in_dim(ht, (1 - core) * half, half, 0)
    t_own = keep + swap(give, "core")
    t_own = t_own + swap(t_own, "z1")
    t_sib = swap(t_own, "z2")
    rest = jnp.concatenate([hw[: 2 * WB, 2 * R :], hw[2 * WB :]], axis=1)
    rest = gather(rest, ("z2", "cols")).reshape(2, GROUPS, 2 * WB, 6 * R)

    inv, a_own = call(first_kernel, [(R, R), (R, R)], "first", True)(side, crit)
    a_sib = swap(a_own, "z4")
    own, c0 = call(first_update_kernel, [(3 * R + half, 3 * R), (3 * R + half, R)], "first_update", True)(
        side, inv, crit, rest, t_own, t_sib
    )
    sib = swap(own, "z4")
    wt = after(columns[:, tgt:], inv).T
    basis = gather(wt, "cols")

    inv = call(inverse_kernel, [(R, R)], "inverse1")(a_own, a_sib)
    own, c1 = call(update_kernel, [(2 * R + half, 2 * R), (2 * R + half, R)], "update1")(inv, own, sib)
    a_own = own[:R, :R]
    a_sib = swap(a_own, "x1")
    sib = swap(own, "x1")
    inv = call(inverse_kernel, [(R, R)], "inverse2")(a_own, a_sib)
    own, c2 = call(update_kernel, [(R + half, R), (R + half, R)], "update2")(inv, own, sib)
    a_own, t_own = own[:R], own[R:]
    a_sib = swap(a_own, "x2")
    t_sib = swap(t_own, "x2")
    k = call(total_kernel, [(half, LEVELS * R)], "total")(a_own, a_sib, t_own, t_sib, c0, c1, c2)
    k_sib = swap(k, "core")
    return call(final_kernel, [(rows, tgt)], "final", True)(core.astype(jnp.int32)[None], columns, basis, k, k_sib)


def solution(mesh):
    fine = Mesh(mesh.devices.reshape(2, 2, 2, 2, 2, 2, GROUPS), (*ROW_AXES, "cols"))
    placed = (P(ROW_AXES, "cols"), P(None, ROW_AXES, None), P(ROW_AXES, None))
    return jax.shard_map(on_device, mesh=fine, in_specs=placed, out_specs=P(ROW_AXES, "cols"), check_vma=False)
```

```python
import functools
import math

import jax
import jax.numpy as jnp
from jax import lax
from jax.experimental import pallas as pl
from jax.experimental.pallas import tpu as pltpu
from jax.sharding import Mesh, PartitionSpec as P


R = 128
LEVELS = 4
WB = 16
GROUPS = 8
ROW_AXES = ("x2", "x1", "z4", "z2", "z1", "core")
HIGH = lax.Precision.HIGHEST
F32 = jnp.float32
BF16 = jnp.bfloat16


def halves(x):
    hi = x.astype(BF16)
    return hi, (x - hi.astype(F32)).astype(BF16)


def mm(a, b):
    dot = functools.partial(jnp.dot, preferred_element_type=F32)
    return dot(a[0], b[0]) + (dot(a[0], b[1]) + dot(a[1], b[0]))


def exact(a, b, dims):
    return lax.dot_general(a, b, ((dims[0], dims[1]), ((), ())), precision=HIGH, preferred_element_type=F32)


def spd_inverse(g):
    lane = lax.broadcasted_iota(jnp.int32, (8, R), 1)
    sub = lax.broadcasted_iota(jnp.int32, (8, R), 0)
    n = R // 8
    tiles = [g[8 * i : 8 * i + 8, :] for i in range(n)]
    full = lambda v: jnp.broadcast_to(v, (8, R))
    for k in range(0, R, 4):
        p, s = k // 8, k % 8
        cols = [[full(tiles[i][:, k + j : k + j + 1]) for i in range(n)] for j in range(4)]
        panel = (lane >= k) & (lane < k + 4)
        rows = [
            jnp.where(lane == k + j, 1.0, jnp.where(panel, 0.0, full(tiles[p][s + j : s + j + 1, :])))
            for j in range(4)
        ]
        d = [[full(cols[j][p][s + i : s + i + 1, :]) for j in range(4)] for i in range(4)]
        r = 1.0 / (d[0][0] * d[1][1] - d[0][1] * d[1][0])
        p00, p01, p10, p11 = d[1][1] * r, -d[0][1] * r, -d[1][0] * r, d[0][0] * r
        e = [
            [p00 * d[0][2] + p01 * d[1][2], p00 * d[0][3] + p01 * d[1][3]],
            [p10 * d[0][2] + p11 * d[1][2], p10 * d[0][3] + p11 * d[1][3]],
        ]
        c = [
            [d[2 + i][2 + j] - (d[2 + i][0] * e[0][j] + d[2 + i][1] * e[1][j]) for j in range(2)]
            for i in range(2)
        ]
        q = 1.0 / (c[0][0] * c[1][1] - c[0][1] * c[1][0])
        t0 = p00 * rows[0] + p01 * rows[1]
        t1 = p10 * rows[0] + p11 * rows[1]
        u0 = rows[2] - (d[2][0] * t0 + d[2][1] * t1)
        u1 = rows[3] - (d[3][0] * t0 + d[3][1] * t1)
        v0 = (c[1][1] * u0 - c[0][1] * u1) * q
        v1 = (c[0][0] * u1 - c[1][0] * u0) * q
        new = [t0 - (e[0][0] * v0 + e[0][1] * v1), t1 - (e[1][0] * v0 + e[1][1] * v1), v0, v1]
        for i in range(n):
            a = jnp.where(panel, 0.0, tiles[i])
            for j in range(4):
                a = a - cols[j][i] * new[j]
            if i == p:
                for j in range(4):
                    a = jnp.where(sub == s + j, new[j], a)
            tiles[i] = a
    return jnp.concatenate(tiles, axis=0)


def pair_inverse(own, sib):
    i = lax.broadcasted_iota(jnp.int32, (R, R), 0)
    j = lax.broadcasted_iota(jnp.int32, (R, R), 1)
    m = jnp.where(i == j, 1.0, 0.0) - exact(own, sib, ((1,), (0,)))
    return exact(spd_inverse(exact(m, m, ((0,), (0,)))), m, ((1,), (1,)))


def coefficients(p_own, p_sib, a_own, a_sib, inv):
    c_own = mm(halves(p_sib - mm(halves(p_own), a_sib)), inv)
    c_own_h = halves(c_own)
    c_sib_h = halves(p_own - mm(c_own_h, a_own))
    return c_own, c_own_h, c_sib_h


def project_kernel(core_ref, order_ref, x_ref, v_ref, scale, xt_ref, w0_ref, keep_ref, give_ref):
    rows, width = x_ref.shape
    tgt = width - LEVELS * WB
    half = tgt // 2
    core = core_ref[0]
    xt = x_ref[...].T
    xt_ref[...] = xt
    hi, lo = halves(xt)
    at = lax.broadcasted_iota(jnp.int32, (rows, rows), 0)
    onehot = jnp.where(at == order_ref[...], 1.0, 0.0).astype(BF16)
    hi = jnp.dot(hi, onehot, preferred_element_type=F32).astype(BF16)
    lo = jnp.dot(lo, onehot, preferred_element_type=F32).astype(BF16)
    later = slice(tgt, width - WB)
    for level in range(LEVELS):
        lanes = slice(R * level, R * level + R)
        h = mm((hi, lo), halves(v_ref[level])) * scale[level]
        keep_ref[:half, lanes] = jnp.where(core == 0, h[:half], h[half:tgt])
        give_ref[:half, lanes] = jnp.where(core == 0, h[half:tgt], h[:half])
        keep_ref[half:, lanes] = h[later]
        give_ref[half:, lanes] = h[later]
        w0_ref[:, :, lanes] = jnp.broadcast_to(h[width - WB :][None], (w0_ref.shape[0], WB, R))


def leaf_sum_kernel(parts_ref, out_ref):
    total = (parts_ref[0] + parts_ref[1]) + (parts_ref[2] + parts_ref[3])
    out_ref[...] = jnp.broadcast_to(total[None], out_ref.shape)


def block(ref, side, rows, lanes):
    part = ref[side, :, rows, lanes]
    return part.reshape(GROUPS * WB, part.shape[-1])


def inverse_kernel(side_ref, g_ref, inv_ref):
    own = side_ref[0]
    rows = g_ref.shape[2]
    last = slice(rows - WB, rows)
    inv_ref[...] = pair_inverse(block(g_ref, own, last, slice(0, R)), block(g_ref, 1 - own, last, slice(0, R)))


def advance(top_own, top_sib, low_own, low_sib, inv):
    a_own, a_sib = halves(top_own[:, :R]), halves(top_sib[:, :R])
    c, c_own, c_sib = coefficients(low_own[:, :R], low_sib[:, :R], a_own, a_sib, halves(inv))
    return c, (low_own[:, R:] + low_sib[:, R:]) - (
        mm(c_own, halves(top_own[:, R:])) + mm(c_sib, halves(top_sib[:, R:]))
    )


def update0_kernel(side_ref, inv_ref, g_ref, q_own_ref, q_sib_ref, q_ref, c_ref, send_ref):
    own, sib = side_ref[0], 1 - side_ref[0]
    every, whole = slice(0, WB), slice(0, LEVELS * R)
    c, q = advance(
        block(g_ref, own, every, whole), block(g_ref, sib, every, whole), q_own_ref[...], q_sib_ref[...], inv_ref[...]
    )
    left = q_ref.shape[0]
    q_ref[...] = q[:left]
    c_ref[...] = c[:left]
    send = jnp.concatenate([q[left:], c[left:]], axis=1)
    send_ref[...] = jnp.broadcast_to(send[None], send_ref.shape)


def update1_kernel(side_ref, inv_ref, g_ref, q_own_ref, q_sib_ref, q_ref, c_ref):
    own, sib = side_ref[0], 1 - side_ref[0]
    lanes = slice(0, q_own_ref.shape[1])
    at = lambda side, m: block(g_ref, side, slice((3 - m) * WB, (4 - m) * WB), lanes)
    low_own = jnp.concatenate([at(own, 2), at(own, 3), q_own_ref[...]], axis=0)
    low_sib = jnp.concatenate([at(sib, 2), at(sib, 3), q_sib_ref[...]], axis=0)
    c_ref[...], q_ref[...] = advance(at(own, 1), at(sib, 1), low_own, low_sib, inv_ref[...])


def level2_kernel(own_ref, sib_ref, q_ref, c_ref):
    own, sib = own_ref[...], sib_ref[...]
    inv = pair_inverse(own[:R, :R], sib[:R, :R])
    c_ref[...], q_ref[...] = advance(own[:R], sib[:R], own[R:], sib[R:], inv)


def total_kernel(side_ref, own_ref, sib_ref, c0_ref, c1_ref, c2_ref, g_ref, k_ref):
    a_own, a_sib = own_ref[:R], sib_ref[:R]
    inv = pair_inverse(a_own, a_sib)
    k3, k3h, _ = coefficients(own_ref[R:], sib_ref[R:], halves(a_own), halves(a_sib), halves(inv))
    w0 = lambda m: halves(block(g_ref, side_ref[0], slice((3 - m) * WB, (4 - m) * WB), slice(3 * R, 4 * R)))
    k2 = c2_ref[R:] - mm(k3h, halves(c2_ref[:R]))
    k2h = halves(k2)
    k1 = c1_ref[2 * R :] - (mm(k2h, halves(c1_ref[:R])) + mm(k3h, halves(c1_ref[R : 2 * R])))
    k1h = halves(k1)
    k0 = c0_ref[...] - (mm(k1h, w0(1)) + mm(k2h, w0(2)) + mm(k3h, w0(3)))
    for level, k in enumerate((k0, k1, k2, k3)):
        k_ref[:, R * level : R * level + R] = k


def final_kernel(core_ref, xt_ref, w_ref, k_own_ref, k_sib_ref, out_ref):
    tgt, rows = out_ref.shape
    core = core_ref[0]
    own, sib = k_own_ref[...], k_sib_ref[...]
    k = halves(jnp.concatenate([jnp.where(core == 0, own, sib), jnp.where(core == 0, sib, own)], axis=0))
    at = [(LEVELS - 1 - level) * WB for level in range(LEVELS)]
    w = halves(jnp.concatenate([w_ref[:, a : a + WB, :].reshape(GROUPS * WB, rows) for a in at], axis=0))
    out_ref[...] = xt_ref[:tgt] - mm(k, w)


def call(kernel, outs, scalars=0):
    shapes = [jax.ShapeDtypeStruct(s, F32) for s in outs]
    single = len(shapes) == 1
    vmem, smem = pl.BlockSpec(memory_space=pltpu.VMEM), pl.BlockSpec(memory_space=pltpu.SMEM)

    def run(*args):
        return pl.pallas_call(
            kernel,
            out_shape=shapes[0] if single else shapes,
            in_specs=[smem] * scalars + [vmem] * (len(args) - scalars),
            out_specs=vmem if single else [vmem] * len(shapes),
            compiler_params=pltpu.CompilerParams(vmem_limit_bytes=56 * 2**20),
        )(*args)

    return run


def swap(v, axis):
    return lax.ppermute(v, axis, [(0, 1), (1, 0)])


def mirror(v, axes):
    n = lax.axis_size(axes)
    return lax.ppermute(v, axes, [(i, n - 1 - i) for i in range(n)])


def exchange(v, axes):
    return lax.all_to_all(v, axes, 0, 0, tiled=True).reshape(2, GROUPS, *v.shape[1:])


def mirror_exchange(v, axes):
    n = lax.axis_size(axes)
    pairs = [[p * GROUPS + y for p in (a, n - 1 - a) for y in range(GROUPS)] for a in range(n // 2)]
    out = lax.all_to_all(v, (*axes, "cols"), 0, 0, tiled=True, axis_index_groups=pairs)
    return out.reshape(2, GROUPS, *v.shape[1:])


Z, X = ("z4", "z2", "z1"), ("x2", "x1")


def sweep(columns, row_bases, order):
    rows, width = columns.shape
    tgt = width - LEVELS * WB
    half = tgt // 2
    wide = LEVELS * R
    scale = [0.55 / math.sqrt(R * rows * (4 << level)) for level in range(LEVELS)]
    index = lambda axis: lax.axis_index(axis).astype(jnp.int32)[None]
    core = index("core")
    sides = [index(axis) for axis in ("z2", "z4")]

    def project(core_ref, order_ref, x_ref, v_ref, *outs):
        project_kernel(core_ref, order_ref, x_ref, v_ref, scale, *outs)

    early = half + (LEVELS - 1) * WB
    xt, w0, keep, give = call(
        project, [(width, rows), (4, WB, wide), (early, wide), (early, wide)], 1
    )(core, order, columns, row_bases)

    q = keep + swap(give, "core")
    w0 = lax.all_to_all(lax.optimization_barrier((w0, q))[0], ("z1", "core"), 0, 0, tiled=True)
    send = call(leaf_sum_kernel, [(2 * GROUPS, WB, wide)])(w0)
    g = exchange(send, ("z2", "cols"))
    q = q + swap(q, "z1")
    q_sib = swap(q, "z2")
    basis = lax.all_to_all(
        jnp.broadcast_to(xt[None, tgt:], (GROUPS, LEVELS * WB, rows)), "cols", 0, 0, tiled=True
    )

    inv = call(inverse_kernel, [(R, R)], 1)(sides[0], g)
    q, c0, send = call(
        update0_kernel, [(half, 3 * R), (half, R), (2 * GROUPS, (LEVELS - 1) * WB, wide)], 1
    )(sides[0], inv, g, q, q_sib)
    g = mirror_exchange(send, Z)
    q_sib = mirror(q, Z)

    inv = call(inverse_kernel, [(R, R)], 1)(sides[1], g)
    q, c1 = call(update1_kernel, [(2 * R + half, 2 * R), (2 * R + half, R)], 1)(sides[1], inv, g, q, q_sib)
    q_sib = swap(q, "x1")
    q, c2 = call(level2_kernel, [(R + half, R), (R + half, R)])(q, q_sib)
    q_sib = mirror(q, X)
    k = call(total_kernel, [(half, wide)], 1)(sides[1], q, q_sib, c0, c1, c2, g)
    k_sib = swap(k, "core")
    return call(final_kernel, [(tgt, rows)], 1)(core, xt, basis, k, k_sib).T


def solution(mesh):
    fine = Mesh(mesh.devices.reshape(2, 2, 2, 2, 2, 2, GROUPS), (*ROW_AXES, "cols"))
    placed = (P(ROW_AXES, "cols"), P(None, ROW_AXES, None), P(ROW_AXES, None))
    return jax.shard_map(sweep, mesh=fine, in_specs=placed, out_specs=P(ROW_AXES, "cols"), check_vma=False)
```

```python
import functools
import math

import jax
import jax.numpy as jnp
from jax import lax
from jax.experimental import pallas as pl
from jax.experimental.pallas import tpu as pltpu
from jax.sharding import Mesh, PartitionSpec as P


R = 128
LEVELS = 4
WB = 16
GROUPS = 8
RING = (1, -1, 2, -2, 3, -3, 4)
ROW_AXES = ("x2", "x1", "z4", "z2", "z1", "core")
HIGH = lax.Precision.HIGHEST
F32 = jnp.float32
BF16 = jnp.bfloat16


def halves(x):
    hi = x.astype(BF16)
    return hi, (x - hi.astype(F32)).astype(BF16)


def mm(a, b):
    dot = functools.partial(jnp.dot, preferred_element_type=F32)
    return dot(a[0], b[0]) + (dot(a[0], b[1]) + dot(a[1], b[0]))


def exact(a, b, dims):
    return lax.dot_general(a, b, ((dims[0], dims[1]), ((), ())), precision=HIGH, preferred_element_type=F32)


def spd_inverse(g):
    lane = lax.broadcasted_iota(jnp.int32, (8, R), 1)
    sub = lax.broadcasted_iota(jnp.int32, (8, R), 0)
    n = R // 8
    tiles = [g[8 * i : 8 * i + 8, :] for i in range(n)]
    full = lambda v: jnp.broadcast_to(v, (8, R))
    for k in range(0, R, 4):
        p, s = k // 8, k % 8
        cols = [[full(tiles[i][:, k + j : k + j + 1]) for i in range(n)] for j in range(4)]
        panel = (lane >= k) & (lane < k + 4)
        rows = [
            jnp.where(lane == k + j, 1.0, jnp.where(panel, 0.0, full(tiles[p][s + j : s + j + 1, :])))
            for j in range(4)
        ]
        d = [[full(cols[j][p][s + i : s + i + 1, :]) for j in range(4)] for i in range(4)]
        r = 1.0 / (d[0][0] * d[1][1] - d[0][1] * d[1][0])
        p00, p01, p10, p11 = d[1][1] * r, -d[0][1] * r, -d[1][0] * r, d[0][0] * r
        e = [
            [p00 * d[0][2] + p01 * d[1][2], p00 * d[0][3] + p01 * d[1][3]],
            [p10 * d[0][2] + p11 * d[1][2], p10 * d[0][3] + p11 * d[1][3]],
        ]
        c = [
            [d[2 + i][2 + j] - (d[2 + i][0] * e[0][j] + d[2 + i][1] * e[1][j]) for j in range(2)]
            for i in range(2)
        ]
        q = 1.0 / (c[0][0] * c[1][1] - c[0][1] * c[1][0])
        t0 = p00 * rows[0] + p01 * rows[1]
        t1 = p10 * rows[0] + p11 * rows[1]
        u0 = rows[2] - (d[2][0] * t0 + d[2][1] * t1)
        u1 = rows[3] - (d[3][0] * t0 + d[3][1] * t1)
        v0 = (c[1][1] * u0 - c[0][1] * u1) * q
        v1 = (c[0][0] * u1 - c[1][0] * u0) * q
        new = [t0 - (e[0][0] * v0 + e[0][1] * v1), t1 - (e[1][0] * v0 + e[1][1] * v1), v0, v1]
        for i in range(n):
            a = jnp.where(panel, 0.0, tiles[i])
            for j in range(4):
                a = a - cols[j][i] * new[j]
            if i == p:
                for j in range(4):
                    a = jnp.where(sub == s + j, new[j], a)
            tiles[i] = a
    return jnp.concatenate(tiles, axis=0)


def pair_inverse(own, sib):
    i = lax.broadcasted_iota(jnp.int32, (R, R), 0)
    j = lax.broadcasted_iota(jnp.int32, (R, R), 1)
    m = jnp.where(i == j, 1.0, 0.0) - exact(own, sib, ((1,), (0,)))
    return exact(spd_inverse(exact(m, m, ((0,), (0,)))), m, ((1,), (1,)))


def coefficients(p_own, p_sib, a_own, a_sib, inv):
    c_own = mm(halves(p_sib - mm(halves(p_own), a_sib)), inv)
    c_own_h = halves(c_own)
    c_sib_h = halves(p_own - mm(c_own_h, a_own))
    return c_own, c_own_h, c_sib_h


def project_kernel(core_ref, order_ref, x_ref, v_ref, scale, xt_ref, w0_ref, keep_ref, give_ref):
    rows, width = x_ref.shape
    tgt = width - LEVELS * WB
    half = tgt // 2
    core = core_ref[0]
    xt = x_ref[...].T
    xt_ref[...] = xt
    hi, lo = halves(xt)
    at = lax.broadcasted_iota(jnp.int32, (rows, rows), 0)
    onehot = jnp.where(at == order_ref[...], 1.0, 0.0).astype(BF16)
    hi = jnp.dot(hi, onehot, preferred_element_type=F32).astype(BF16)
    lo = jnp.dot(lo, onehot, preferred_element_type=F32).astype(BF16)
    later = slice(tgt, width - WB)
    for level in range(LEVELS):
        lanes = slice(R * level, R * level + R)
        h = mm((hi, lo), halves(v_ref[level])) * scale[level]
        keep_ref[:half, lanes] = jnp.where(core == 0, h[:half], h[half:tgt])
        give_ref[:half, lanes] = jnp.where(core == 0, h[half:tgt], h[:half])
        keep_ref[half:, lanes] = h[later]
        give_ref[half:, lanes] = h[later]
        w0_ref[:, :, lanes] = jnp.broadcast_to(h[width - WB :][None], (w0_ref.shape[0], WB, R))


def leaf_sum_kernel(parts_ref, out_ref):
    total = (parts_ref[0] + parts_ref[1]) + (parts_ref[2] + parts_ref[3])
    out_ref[...] = jnp.broadcast_to(total[None], out_ref.shape)


def block(ref, side, rows, lanes):
    part = ref[side, :, rows, lanes]
    return part.reshape(GROUPS * WB, part.shape[-1])


def couple(g_ref, side, lanes):
    rows = g_ref.shape[2]
    return block(g_ref, side, slice(rows - WB, rows), lanes)


def inverse_kernel(side_ref, g_ref, inv_ref):
    own = side_ref[0]
    inv_ref[...] = pair_inverse(couple(g_ref, own, slice(0, R)), couple(g_ref, 1 - own, slice(0, R)))


def last_inverse_kernel(own_ref, sib_ref, inv_ref):
    inv_ref[...] = pair_inverse(own_ref[...], sib_ref[...])


def advance(top_own, top_sib, low_own, low_sib, inv):
    a_own, a_sib = halves(top_own[:, :R]), halves(top_sib[:, :R])
    c, c_own, c_sib = coefficients(low_own[:, :R], low_sib[:, :R], a_own, a_sib, halves(inv))
    return c, (low_own[:, R:] + low_sib[:, R:]) - (
        mm(c_own, halves(top_own[:, R:])) + mm(c_sib, halves(top_sib[:, R:]))
    )


def basis_kernel(side_ref, inv_ref, g_ref, w_own_ref, w_sib_ref, *refs):
    c_ref, send_ref = refs[-2:]
    own, whole = side_ref[0], slice(0, g_ref.shape[3])
    c, w = advance(
        couple(g_ref, own, whole), couple(g_ref, 1 - own, whole), w_own_ref[...], w_sib_ref[...], inv_ref[...]
    )
    c_ref[...] = c
    left = w.shape[0] - send_ref.shape[1]
    if left:
        refs[0][...] = w[:left]
    send_ref[...] = jnp.broadcast_to(w[left:][None], send_ref.shape)


def last_basis_kernel(side_ref, inv_ref, g_ref, a_ref, c_ref):
    own, whole, first = side_ref[0], slice(0, g_ref.shape[3]), slice(0, WB)
    c_ref[...], a_ref[...] = advance(
        couple(g_ref, own, whole),
        couple(g_ref, 1 - own, whole),
        block(g_ref, own, first, whole),
        block(g_ref, 1 - own, first, whole),
        inv_ref[...],
    )


def targets_kernel(side_ref, inv_ref, g_ref, t_own_ref, t_sib_ref, t_ref, c_ref):
    own, whole = side_ref[0], slice(0, g_ref.shape[3])
    c_ref[...], t_ref[...] = advance(
        couple(g_ref, own, whole), couple(g_ref, 1 - own, whole), t_own_ref[...], t_sib_ref[...], inv_ref[...]
    )


def total_kernel(inv_ref, a_own_ref, a_sib_ref, t_own_ref, t_sib_ref, t0_ref, t1_ref, t2_ref, w2_ref, cw_ref, k_ref):
    k3, k3h, _ = coefficients(
        t_own_ref[...], t_sib_ref[...], halves(a_own_ref[...]), halves(a_sib_ref[...]), halves(inv_ref[...])
    )
    w = lambda i: halves(cw_ref[:, i * WB : i * WB + WB, :].reshape(GROUPS * WB, R))
    k2 = t2_ref[...] - mm(k3h, halves(w2_ref[...]))
    k2h = halves(k2)
    k1 = t1_ref[...] - (mm(k2h, w(4)) + mm(k3h, w(3)))
    k1h = halves(k1)
    k0 = t0_ref[...] - (mm(k1h, w(2)) + mm(k2h, w(1)) + mm(k3h, w(0)))
    for level, k in enumerate((k0, k1, k2, k3)):
        k_ref[:, R * level : R * level + R] = k


def final_kernel(core_ref, col_ref, xt_ref, *refs):
    part_refs, (k_own_ref, k_sib_ref, out_ref, w_ref) = refs[: GROUPS - 1], refs[GROUPS - 1 :]
    tgt, rows = out_ref.shape
    core, col = core_ref[0], col_ref[0]
    w_ref[col] = xt_ref[tgt:]
    for shift, part_ref in zip(RING, part_refs):
        w_ref[lax.rem(col + (shift + GROUPS), GROUPS)] = part_ref[...]
    own, sib = k_own_ref[...], k_sib_ref[...]
    k = halves(jnp.concatenate([jnp.where(core == 0, own, sib), jnp.where(core == 0, sib, own)], axis=0))
    at = [(LEVELS - 1 - level) * WB for level in range(LEVELS)]
    w = halves(jnp.concatenate([w_ref[:, a : a + WB, :].reshape(GROUPS * WB, rows) for a in at], axis=0))
    out_ref[...] = xt_ref[:tgt] - mm(k, w)


def call(kernel, outs, scalars=0, scratch=()):
    shapes = [jax.ShapeDtypeStruct(s, F32) for s in outs]
    single = len(shapes) == 1
    vmem, smem = pl.BlockSpec(memory_space=pltpu.VMEM), pl.BlockSpec(memory_space=pltpu.SMEM)

    def run(*args):
        return pl.pallas_call(
            kernel,
            out_shape=shapes[0] if single else shapes,
            in_specs=[smem] * scalars + [vmem] * (len(args) - scalars),
            out_specs=vmem if single else [vmem] * len(shapes),
            scratch_shapes=[pltpu.VMEM(shape, F32) for shape in scratch],
            compiler_params=pltpu.CompilerParams(vmem_limit_bytes=56 * 2**20),
        )(*args)

    return run


def swap(v, axis):
    return lax.ppermute(v, axis, [(0, 1), (1, 0)])


def mirror(v, axes):
    n = lax.axis_size(axes)
    return lax.ppermute(v, axes, [(i, n - 1 - i) for i in range(n)])


def exchange(v, axes):
    return lax.all_to_all(v, axes, 0, 0, tiled=True).reshape(2, GROUPS, *v.shape[1:])


def mirror_exchange(v, axes):
    n = lax.axis_size(axes)
    pairs = [[p * GROUPS + y for p in (a, n - 1 - a) for y in range(GROUPS)] for a in range(n // 2)]
    out = lax.all_to_all(v, (*axes, "cols"), 0, 0, tiled=True, axis_index_groups=pairs)
    return out.reshape(2, GROUPS, *v.shape[1:])


Z, X = ("z4", "z2", "z1"), ("x2", "x1")


def sweep(columns, row_bases, order):
    rows, width = columns.shape
    tgt = width - LEVELS * WB
    half = tgt // 2
    wide = LEVELS * R
    scale = [0.55 / math.sqrt(R * rows * (4 << level)) for level in range(LEVELS)]
    index = lambda axis: lax.axis_index(axis).astype(jnp.int32)[None]
    core = index("core")
    sides = [index(axis) for axis in ("z2", "z4", "x1")]

    def project(core_ref, order_ref, x_ref, v_ref, *outs):
        project_kernel(core_ref, order_ref, x_ref, v_ref, scale, *outs)

    early = half + (LEVELS - 1) * WB
    xt, w0, keep, give = call(
        project, [(width, rows), (4, WB, wide), (early, wide), (early, wide)], 1
    )(core, order, columns, row_bases)

    q = keep + swap(give, "core")
    w0 = lax.all_to_all(lax.optimization_barrier((w0, q))[0], ("z1", "core"), 0, 0, tiled=True)
    moved = swap(q, "z1")
    t, w = q[:half] + moved[:half], q[half:] + moved[half:]
    send = call(leaf_sum_kernel, [(2 * GROUPS, WB, wide)])(w0)
    g0 = exchange(send, ("z2", "cols"))
    w_sib = swap(w, "z2")
    t_sib = swap(t, "z2")

    parts, held = [], {1: xt[tgt:], -1: xt[tgt:]}
    for shift in RING:
        way = 1 if shift > 0 else -1
        held[way] = lax.ppermute(held[way], "cols", [((y + way) % GROUPS, y) for y in range(GROUPS)])
        parts.append(held[way])

    inv0 = call(inverse_kernel, [(R, R)], 1)(sides[0], g0)
    w, cw0, send = call(
        basis_kernel, [(2 * WB, 3 * R), (3 * WB, R), (2 * GROUPS, WB, 3 * R)], 1
    )(sides[0], inv0, g0, w, w_sib)
    g1 = mirror_exchange(send, Z)
    w_sib = mirror(w, Z)
    t, t0 = call(targets_kernel, [(half, 3 * R), (half, R)], 1)(sides[0], inv0, g0, t, t_sib)
    t_sib = mirror(t, Z)

    inv1 = call(inverse_kernel, [(R, R)], 1)(sides[1], g1)
    cw1, send = call(basis_kernel, [(2 * WB, R), (2 * GROUPS, 2 * WB, 2 * R)], 1)(sides[1], inv1, g1, w, w_sib)
    g2 = exchange(send, ("x1", "cols"))
    t, t1 = call(targets_kernel, [(half, 2 * R), (half, R)], 1)(sides[1], inv1, g1, t, t_sib)
    t_sib = swap(t, "x1")

    inv2 = call(inverse_kernel, [(R, R)], 1)(sides[2], g2)
    a3, cw2 = call(last_basis_kernel, [(R, R), (R, R)], 1)(sides[2], inv2, g2)
    a3_sib = mirror(a3, X)
    cw = jnp.concatenate([cw0, cw1], axis=0)
    cw = lax.all_to_all(jnp.broadcast_to(cw[None], (GROUPS, *cw.shape)), "cols", 0, 0, tiled=True)
    t, t2 = call(targets_kernel, [(half, R), (half, R)], 1)(sides[2], inv2, g2, t, t_sib)
    t_sib = mirror(t, X)

    inv3 = call(last_inverse_kernel, [(R, R)])(a3, a3_sib)
    k = call(total_kernel, [(half, wide)])(inv3, a3, a3_sib, t, t_sib, t0, t1, t2, cw2, cw)
    k_sib = swap(k, "core")
    return call(final_kernel, [(tgt, rows)], 2, [(GROUPS, LEVELS * WB, rows)])(
        core, index("cols"), xt, *parts, k, k_sib
    ).T


def solution(mesh):
    fine = Mesh(mesh.devices.reshape(2, 2, 2, 2, 2, 2, GROUPS), (*ROW_AXES, "cols"))
    placed = (P(ROW_AXES, "cols"), P(None, ROW_AXES, None), P(ROW_AXES, None))
    return jax.shard_map(sweep, mesh=fine, in_specs=placed, out_specs=P(ROW_AXES, "cols"), check_vma=False)
```

```python
import functools
import math

import jax
import jax.numpy as jnp
from jax import lax
from jax.experimental import pallas as pl
from jax.experimental.pallas import tpu as pltpu
from jax.sharding import Mesh, PartitionSpec as P


R = 128
LEVELS = 4
WB = 16
GROUPS = 8
RING = (1, -1, 2, -2, 3, -3, 4)
ROW_AXES = ("x2", "x1", "z4", "z2", "z1", "core")
HIGH = lax.Precision.HIGHEST
F32 = jnp.float32
BF16 = jnp.bfloat16


def halves(x):
    hi = x.astype(BF16)
    return hi, (x - hi.astype(F32)).astype(BF16)


def mm(a, b):
    dot = functools.partial(jnp.dot, preferred_element_type=F32)
    return dot(a[0], b[0]) + (dot(a[0], b[1]) + dot(a[1], b[0]))


def exact(a, b, dims):
    return lax.dot_general(a, b, ((dims[0], dims[1]), ((), ())), precision=HIGH, preferred_element_type=F32)


def spd_inverse(g):
    lane = lax.broadcasted_iota(jnp.int32, (8, R), 1)
    sub = lax.broadcasted_iota(jnp.int32, (8, R), 0)
    n = R // 8
    tiles = [g[8 * i : 8 * i + 8, :] for i in range(n)]
    full = lambda v: jnp.broadcast_to(v, (8, R))
    row = lambda v, i: full(v[i : i + 1, :])
    for p in range(n):
        k = 8 * p
        cols = [[full(tiles[i][:, k + j : k + j + 1]) for i in range(n)] for j in range(8)]
        panel = (lane >= k) & (lane < k + 8)
        rows = jnp.where(panel, jnp.where(lane == sub + k, 1.0, 0.0), tiles[p])
        d = [cols[j][p] for j in range(8)]
        for s in range(0, 8, 2):
            a, b, c, e = row(d[s], s), row(d[s + 1], s), row(d[s], s + 1), row(d[s + 1], s + 1)
            r = 1.0 / (a * e - b * c)
            p00, p01, p10, p11 = e * r, -b * r, -c * r, a * r
            f0, f1 = d[s], d[s + 1]

            def step(v):
                b0, b1 = row(v, s), row(v, s + 1)
                n0, n1 = p00 * b0 + p01 * b1, p10 * b0 + p11 * b1
                return jnp.where(sub == s, n0, jnp.where(sub == s + 1, n1, v - f0 * n0 - f1 * n1))

            for j in range(s + 2, 8):
                d[j] = step(d[j])
            rows = step(rows)
        new = [row(rows, j) for j in range(8)]
        for i in range(n):
            if i != p:
                t = jnp.where(panel, 0.0, tiles[i])
                for j in range(8):
                    t = t - cols[j][i] * new[j]
                tiles[i] = t
        tiles[p] = rows
    return jnp.concatenate(tiles, axis=0)


def pair_inverse(own, sib):
    i = lax.broadcasted_iota(jnp.int32, (R, R), 0)
    j = lax.broadcasted_iota(jnp.int32, (R, R), 1)
    m = jnp.where(i == j, 1.0, 0.0) - exact(own, sib, ((1,), (0,)))
    return exact(spd_inverse(exact(m, m, ((0,), (0,)))), m, ((1,), (1,)))


def coefficients(p_own, p_sib, a_own, a_sib, inv):
    c_own = mm(halves(p_sib - mm(halves(p_own), a_sib)), inv)
    c_own_h = halves(c_own)
    c_sib_h = halves(p_own - mm(c_own_h, a_own))
    return c_own, c_own_h, c_sib_h


def project_kernel(core_ref, order_hbm, x_hbm, v_hbm, scale, xt_hbm, wt_ref, w0_ref, keep_ref, give_ref, *scratch):
    order_ref, x_ref, v_ref, xt_ref, sems = scratch
    copies = [
        pltpu.make_async_copy(order_hbm, order_ref, sems.at[0]),
        pltpu.make_async_copy(x_hbm, x_ref, sems.at[1]),
    ] + [pltpu.make_async_copy(v_hbm.at[i], v_ref.at[i], sems.at[2 + i]) for i in range(LEVELS)]
    out = pltpu.make_async_copy(xt_ref, xt_hbm, sems.at[2 + LEVELS])
    copies[0].start()
    copies[1].start()
    rows, width = x_ref.shape
    tgt = width - LEVELS * WB
    half = tgt // 2
    core = core_ref[0]
    copies[0].wait()
    at = lax.broadcasted_iota(jnp.int32, (rows, rows), 0)
    onehot = jnp.where(at == order_ref[...], 1.0, 0.0).astype(BF16)
    copies[1].wait()
    for copy in copies[2:]:
        copy.start()
    xt = x_ref[...].T
    xt_ref[...] = xt[:tgt]
    out.start()
    wt_ref[...] = xt[tgt:]
    hi, lo = halves(xt)
    hi = jnp.dot(hi, onehot, preferred_element_type=F32).astype(BF16)
    lo = jnp.dot(lo, onehot, preferred_element_type=F32).astype(BF16)
    later = slice(tgt, width - WB)
    for level in range(LEVELS):
        lanes = slice(R * level, R * level + R)
        copies[2 + level].wait()
        h = mm((hi, lo), halves(v_ref[level])) * scale[level]
        keep_ref[:half, lanes] = jnp.where(core == 0, h[:half], h[half:tgt])
        give_ref[:half, lanes] = jnp.where(core == 0, h[half:tgt], h[:half])
        keep_ref[half:, lanes] = h[later]
        give_ref[half:, lanes] = h[later]
        w0_ref[:, :, lanes] = jnp.broadcast_to(h[width - WB :][None], (w0_ref.shape[0], WB, R))
    out.wait()


def leaf_sum_kernel(parts_ref, out_ref):
    total = (parts_ref[0] + parts_ref[1]) + (parts_ref[2] + parts_ref[3])
    out_ref[...] = jnp.broadcast_to(total[None], out_ref.shape)


def block(ref, side, rows, lanes):
    part = ref[side, :, rows, lanes]
    return part.reshape(GROUPS * WB, part.shape[-1])


def couple(g_ref, side, lanes):
    rows = g_ref.shape[2]
    return block(g_ref, side, slice(rows - WB, rows), lanes)


def inverse_kernel(side_ref, g_ref, inv_ref):
    own = side_ref[0]
    inv_ref[...] = pair_inverse(couple(g_ref, own, slice(0, R)), couple(g_ref, 1 - own, slice(0, R)))


def last_inverse_kernel(own_ref, sib_ref, inv_ref):
    inv_ref[...] = pair_inverse(own_ref[...], sib_ref[...])


def advance(top_own, top_sib, low_own, low_sib, inv):
    a_own, a_sib = halves(top_own[:, :R]), halves(top_sib[:, :R])
    c, c_own, c_sib = coefficients(low_own[:, :R], low_sib[:, :R], a_own, a_sib, halves(inv))
    return c, (low_own[:, R:] + low_sib[:, R:]) - (
        mm(c_own, halves(top_own[:, R:])) + mm(c_sib, halves(top_sib[:, R:]))
    )


def basis0_kernel(side_ref, inv_ref, g_ref, w_own_ref, w_sib_ref, w_ref, c_hbm, send_ref, c_ref, sems):
    own, whole = side_ref[0], slice(0, g_ref.shape[3])
    c_ref[...], w = advance(
        couple(g_ref, own, whole), couple(g_ref, 1 - own, whole), w_own_ref[...], w_sib_ref[...], inv_ref[...]
    )
    out = pltpu.make_async_copy(c_ref, c_hbm, sems.at[0])
    out.start()
    left = w_ref.shape[0]
    w_ref[...] = w[:left]
    send_ref[...] = jnp.broadcast_to(w[left:][None], send_ref.shape)
    out.wait()


def basis1_kernel(side_ref, inv_ref, g_ref, w_own_ref, w_sib_ref, c0_hbm, c_ref, send_ref, c0_ref, sems):
    earlier = pltpu.make_async_copy(c0_hbm, c0_ref, sems.at[0])
    earlier.start()
    own, whole = side_ref[0], slice(0, g_ref.shape[3])
    c, w = advance(
        couple(g_ref, own, whole), couple(g_ref, 1 - own, whole), w_own_ref[...], w_sib_ref[...], inv_ref[...]
    )
    send_ref[...] = jnp.broadcast_to(w[None], send_ref.shape)
    earlier.wait()
    first = c0_ref.shape[0]
    c_ref[:, :first, :] = jnp.broadcast_to(c0_ref[...][None], (GROUPS, first, R))
    c_ref[:, first:, :] = jnp.broadcast_to(c[None], (GROUPS, *c.shape))


def last_basis_kernel(side_ref, inv_ref, g_ref, a_ref, c_hbm, c_ref, sems):
    own, whole, first = side_ref[0], slice(0, g_ref.shape[3]), slice(0, WB)
    c_ref[...], a_ref[...] = advance(
        couple(g_ref, own, whole),
        couple(g_ref, 1 - own, whole),
        block(g_ref, own, first, whole),
        block(g_ref, 1 - own, first, whole),
        inv_ref[...],
    )
    out = pltpu.make_async_copy(c_ref, c_hbm, sems.at[0])
    out.start()
    out.wait()


def targets_kernel(side_ref, inv_ref, g_ref, t_own_ref, t_sib_ref, t_ref, c_hbm, c_ref, sems):
    own, whole = side_ref[0], slice(0, g_ref.shape[3])
    c_ref[...], t = advance(
        couple(g_ref, own, whole), couple(g_ref, 1 - own, whole), t_own_ref[...], t_sib_ref[...], inv_ref[...]
    )
    out = pltpu.make_async_copy(c_ref, c_hbm, sems.at[0])
    out.start()
    t_ref[...] = t
    out.wait()


def split_sum_kernel(q_ref, moved_ref, t_ref, w_ref):
    half = t_ref.shape[0]
    t_ref[...] = q_ref[:half] + moved_ref[:half]
    w_ref[...] = q_ref[half:] + moved_ref[half:]


def total_kernel(inv_ref, a_own_ref, a_sib_ref, t_own_ref, t_sib_ref, *refs):
    far, (cw_ref, k_ref), near, sems = refs[:4], refs[4:6], refs[6:10], refs[10]
    copies = [pltpu.make_async_copy(a, b, sems.at[i]) for i, (a, b) in enumerate(zip(far, near))]
    for copy in copies:
        copy.start()
    t0_ref, t1_ref, t2_ref, w2_ref = near
    k3, k3h, _ = coefficients(
        t_own_ref[...], t_sib_ref[...], halves(a_own_ref[...]), halves(a_sib_ref[...]), halves(inv_ref[...])
    )
    for copy in copies:
        copy.wait()
    w = lambda i: halves(cw_ref[:, i * WB : i * WB + WB, :].reshape(GROUPS * WB, R))
    k2 = t2_ref[...] - mm(k3h, halves(w2_ref[...]))
    k2h = halves(k2)
    k1 = t1_ref[...] - (mm(k2h, w(4)) + mm(k3h, w(3)))
    k1h = halves(k1)
    k0 = t0_ref[...] - (mm(k1h, w(2)) + mm(k2h, w(1)) + mm(k3h, w(0)))
    for level, k in enumerate((k0, k1, k2, k3)):
        k_ref[:, R * level : R * level + R] = k


def final_kernel(core_ref, col_ref, xt_ref, wt_ref, *refs):
    part_refs, (k_own_ref, k_sib_ref, out_hbm, w_ref, out_ref, near_ref, sems) = refs[: GROUPS - 1], refs[GROUPS - 1 :]
    near = pltpu.make_async_copy(xt_ref, near_ref, sems.at[1])
    near.start()
    tgt, rows = out_ref.shape
    core, col = core_ref[0], col_ref[0]
    w_ref[col] = wt_ref[...]
    for shift, part_ref in zip(RING, part_refs):
        w_ref[lax.rem(col + (shift + GROUPS), GROUPS)] = part_ref[...]
    own, sib = k_own_ref[...], k_sib_ref[...]
    k = halves(jnp.concatenate([jnp.where(core == 0, own, sib), jnp.where(core == 0, sib, own)], axis=0))
    at = [(LEVELS - 1 - level) * WB for level in range(LEVELS)]
    w = halves(jnp.concatenate([w_ref[:, a : a + WB, :].reshape(GROUPS * WB, rows) for a in at], axis=0))
    half = tgt // 2
    outs = []
    for i in range(2):
        part = slice(i * half, i * half + half)
        total = mm((k[0][part], k[1][part]), w)
        if i == 0:
            near.wait()
        out_ref[part] = near_ref[part] - total
        outs.append(pltpu.make_async_copy(out_ref.at[part], out_hbm.at[part], sems.at[2 * i]))
        outs[-1].start()
    for out in outs:
        out.wait()


def call(kernel, outs, scalars=0, scratch=(), far=(), from_hbm=(), limit=16):
    shapes = [pltpu.HBM(s, F32) if i in far else pltpu.VMEM(s, F32) for i, s in enumerate(outs)]
    single = len(shapes) == 1
    vmem, smem = pl.BlockSpec(memory_space=pltpu.VMEM), pl.BlockSpec(memory_space=pltpu.SMEM)
    hbm = pl.BlockSpec(memory_space=pltpu.HBM)

    def run(*args):
        spaces = [None if i < scalars else pltpu.HBM if i in from_hbm else pltpu.VMEM for i in range(len(args))]
        specs = [smem if m is None else hbm if m is pltpu.HBM else vmem for m in spaces]
        through = [outs[i] for i in far] + [args[i].shape for i in from_hbm]
        return pl.pallas_call(
            kernel,
            out_shape=shapes[0] if single else shapes,
            in_specs=specs,
            out_specs=(hbm if far else vmem) if single else [hbm if i in far else vmem for i in range(len(outs))],
            scratch_shapes=[pltpu.VMEM(shape, F32) for shape in (*scratch, *through)]
            + ([pltpu.SemaphoreType.DMA((len(through) + 1,))] if through else []),
            compiler_params=pltpu.CompilerParams(vmem_limit_bytes=limit * 2**20),
        )(*(a if m is None else pltpu.with_memory_space_constraint(a, m) for a, m in zip(args, spaces)))

    return run


def swap(v, axis):
    return lax.ppermute(v, axis, [(0, 1), (1, 0)])


def mirror(v, axes):
    n = lax.axis_size(axes)
    return lax.ppermute(v, axes, [(i, n - 1 - i) for i in range(n)])


def exchange(v, axes):
    return lax.all_to_all(v, axes, 0, 0, tiled=True).reshape(2, GROUPS, *v.shape[1:])


def mirror_exchange(v, axes):
    n = lax.axis_size(axes)
    pairs = [[p * GROUPS + y for p in (a, n - 1 - a) for y in range(GROUPS)] for a in range(n // 2)]
    out = lax.all_to_all(v, (*axes, "cols"), 0, 0, tiled=True, axis_index_groups=pairs)
    return out.reshape(2, GROUPS, *v.shape[1:])


Z, X = ("z4", "z2", "z1"), ("x2", "x1")


def sweep(columns, row_bases, order):
    rows, width = columns.shape
    tgt = width - LEVELS * WB
    half = tgt // 2
    wide = LEVELS * R
    scale = [0.55 / math.sqrt(R * rows * (4 << level)) for level in range(LEVELS)]
    index = lambda axis: lax.axis_index(axis).astype(jnp.int32)[None]
    core = index("core")
    sides = [index(axis) for axis in ("z2", "z4", "x1")]

    def project(core_ref, order_hbm, x_hbm, v_hbm, *refs):
        project_kernel(core_ref, order_hbm, x_hbm, v_hbm, scale, *refs)

    early = half + (LEVELS - 1) * WB
    hbm, vmem = pl.BlockSpec(memory_space=pltpu.HBM), pl.BlockSpec(memory_space=pltpu.VMEM)
    xt, wt, w0, keep, give = pl.pallas_call(
        project,
        out_shape=[pltpu.HBM((tgt, rows), F32)]
        + [pltpu.VMEM(s, F32) for s in ((LEVELS * WB, rows), (4, WB, wide), (early, wide), (early, wide))],
        in_specs=[pl.BlockSpec(memory_space=pltpu.SMEM), hbm, hbm, hbm],
        out_specs=[hbm] + [vmem] * 4,
        scratch_shapes=[
            pltpu.VMEM(order.shape, jnp.int32),
            pltpu.VMEM(columns.shape, F32),
            pltpu.VMEM(row_bases.shape, F32),
            pltpu.VMEM((tgt, rows), F32),
            pltpu.SemaphoreType.DMA((3 + LEVELS,)),
        ],
        name="project",
        compiler_params=pltpu.CompilerParams(vmem_limit_bytes=40 * 2**20),
    )(core, *(pltpu.with_memory_space_constraint(v, pltpu.HBM) for v in (order, columns, row_bases)))

    q = keep + swap(give, "core")
    w0 = lax.all_to_all(lax.optimization_barrier((w0, q))[0], ("z1", "core"), 0, 0, tiled=True)
    moved = swap(q, "z1")
    t, w = call(split_sum_kernel, [(half, wide), (early - half, wide)])(q, moved)
    send = call(leaf_sum_kernel, [(2 * GROUPS, WB, wide)])(w0)
    g0 = exchange(send, ("z2", "cols"))
    w_sib = swap(w, "z2")
    t_sib = swap(t, "z2")

    parts, held = [], {1: wt, -1: wt}
    for shift in RING:
        way = 1 if shift > 0 else -1
        held[way] = lax.ppermute(held[way], "cols", [((y + way) % GROUPS, y) for y in range(GROUPS)])
        parts.append(held[way])

    inv0 = call(inverse_kernel, [(R, R)], 1)(sides[0], g0)
    w, cw0, send = call(
        basis0_kernel, [(2 * WB, 3 * R), (3 * WB, R), (2 * GROUPS, WB, 3 * R)], 1, far=(1,)
    )(sides[0], inv0, g0, w, w_sib)
    g1 = mirror_exchange(send, Z)
    w_sib = mirror(w, Z)
    t, t0 = call(targets_kernel, [(half, 3 * R), (half, R)], 1, far=(1,))(sides[0], inv0, g0, t, t_sib)
    t_sib = mirror(t, Z)

    inv1 = call(inverse_kernel, [(R, R)], 1)(sides[1], g1)
    cw, send = call(
        basis1_kernel, [(GROUPS, 5 * WB, R), (2 * GROUPS, 2 * WB, 2 * R)], 1, from_hbm=(5,)
    )(sides[1], inv1, g1, w, w_sib, cw0)
    g2 = exchange(send, ("x1", "cols"))
    t, t1 = call(targets_kernel, [(half, 2 * R), (half, R)], 1, far=(1,))(sides[1], inv1, g1, t, t_sib)
    t_sib = swap(t, "x1")

    inv2 = call(inverse_kernel, [(R, R)], 1)(sides[2], g2)
    a3, cw2 = call(last_basis_kernel, [(R, R), (R, R)], 1, far=(1,))(sides[2], inv2, g2)
    a3_sib = mirror(a3, X)
    cw = lax.all_to_all(cw, "cols", 0, 0, tiled=True)
    t, t2 = call(targets_kernel, [(half, R), (half, R)], 1, far=(1,))(sides[2], inv2, g2, t, t_sib)
    t_sib = mirror(t, X)

    inv3 = call(last_inverse_kernel, [(R, R)])(a3, a3_sib)
    k = call(total_kernel, [(half, wide)], from_hbm=(5, 6, 7, 8))(inv3, a3, a3_sib, t, t_sib, t0, t1, t2, cw2, cw)
    k_sib = swap(k, "core")
    return call(final_kernel, [(tgt, rows)], 2, [(GROUPS, LEVELS * WB, rows)], (0,), (2,), 24)(
        core, index("cols"), xt, wt, *parts, k, k_sib
    ).T


def solution(mesh):
    fine = Mesh(mesh.devices.reshape(2, 2, 2, 2, 2, 2, GROUPS), (*ROW_AXES, "cols"))
    placed = (P(ROW_AXES, "cols"), P(None, ROW_AXES, None), P(ROW_AXES, None))
    return jax.shard_map(sweep, mesh=fine, in_specs=placed, out_specs=P(ROW_AXES, "cols"), check_vma=False)
```

```python
import functools
import math

import jax
import jax.numpy as jnp
from jax import lax
from jax.experimental import pallas as pl
from jax.experimental.pallas import tpu as pltpu
from jax.sharding import Mesh, PartitionSpec as P


R = 128
LEVELS = 4
WB = 16
GROUPS = 8
ROW_AXES = ("x2", "x1", "z4", "z2", "z1", "core")
HIGH = lax.Precision.HIGHEST
F32 = jnp.float32
BF16 = jnp.bfloat16


def halves(x):
    hi = x.astype(BF16)
    return hi, (x - hi.astype(F32)).astype(BF16)


def mm(a, b):
    dot = functools.partial(jnp.dot, preferred_element_type=F32)
    return dot(a[0], b[0]) + (dot(a[0], b[1]) + dot(a[1], b[0]))


def exact(a, b, dims):
    return lax.dot_general(a, b, ((dims[0], dims[1]), ((), ())), precision=HIGH, preferred_element_type=F32)


def spd_inverse(g):
    lane = lax.broadcasted_iota(jnp.int32, (8, R), 1)
    sub = lax.broadcasted_iota(jnp.int32, (8, R), 0)
    n = R // 8
    tiles = [g[8 * i : 8 * i + 8, :] for i in range(n)]
    full = lambda v: jnp.broadcast_to(v, (8, R))
    row = lambda v, i: full(v[i : i + 1, :])
    for p in range(n):
        k = 8 * p
        cols = [[full(tiles[i][:, k + j : k + j + 1]) for i in range(n)] for j in range(8)]
        panel = (lane >= k) & (lane < k + 8)
        rows = jnp.where(panel, jnp.where(lane == sub + k, 1.0, 0.0), tiles[p])
        d = [cols[j][p] for j in range(8)]
        for s in range(0, 8, 2):
            a, b, c, e = row(d[s], s), row(d[s + 1], s), row(d[s], s + 1), row(d[s + 1], s + 1)
            r = 1.0 / (a * e - b * c)
            p00, p01, p10, p11 = e * r, -b * r, -c * r, a * r
            f0, f1 = d[s], d[s + 1]

            def step(v):
                b0, b1 = row(v, s), row(v, s + 1)
                n0, n1 = p00 * b0 + p01 * b1, p10 * b0 + p11 * b1
                return jnp.where(sub == s, n0, jnp.where(sub == s + 1, n1, v - f0 * n0 - f1 * n1))

            for j in range(s + 2, 8):
                d[j] = step(d[j])
            rows = step(rows)
        new = [row(rows, j) for j in range(8)]
        for i in range(n):
            if i != p:
                t = jnp.where(panel, 0.0, tiles[i])
                for j in range(8):
                    t = t - cols[j][i] * new[j]
                tiles[i] = t
        tiles[p] = rows
    return jnp.concatenate(tiles, axis=0)


def pair_inverse(own, sib):
    i = lax.broadcasted_iota(jnp.int32, (R, R), 0)
    j = lax.broadcasted_iota(jnp.int32, (R, R), 1)
    m = jnp.where(i == j, 1.0, 0.0) - exact(own, sib, ((1,), (0,)))
    return exact(spd_inverse(exact(m, m, ((0,), (0,)))), m, ((1,), (1,)))


def coefficients(p_own, p_sib, a_own, a_sib, inv):
    c_own = mm(halves(p_sib - mm(halves(p_own), a_sib)), inv)
    c_own_h = halves(c_own)
    c_sib_h = halves(p_own - mm(c_own_h, a_own))
    return c_own, c_own_h, c_sib_h


def project_kernel(core_ref, order_hbm, x_hbm, v_hbm, scale, xt_hbm, wt_ref, w0_ref, keep_ref, give_ref, *scratch):
    order_ref, x_ref, v_ref, xt_ref, sems = scratch
    copies = [
        pltpu.make_async_copy(order_hbm, order_ref, sems.at[0]),
        pltpu.make_async_copy(x_hbm, x_ref, sems.at[1]),
    ] + [pltpu.make_async_copy(v_hbm.at[i], v_ref.at[i], sems.at[2 + i]) for i in range(LEVELS)]
    out = pltpu.make_async_copy(xt_ref, xt_hbm, sems.at[2 + LEVELS])
    copies[0].start()
    copies[1].start()
    rows, width = x_ref.shape
    tgt = width - LEVELS * WB
    half = tgt // 2
    core = core_ref[0]
    copies[0].wait()
    at = lax.broadcasted_iota(jnp.int32, (rows, rows), 0)
    onehot = jnp.where(at == order_ref[...], 1.0, 0.0).astype(BF16)
    copies[1].wait()
    for copy in copies[2:]:
        copy.start()
    xt = x_ref[...].T
    xt_ref[...] = xt[:tgt]
    out.start()
    wt_ref[...] = xt[tgt:]
    hi, lo = halves(xt)
    hi = jnp.dot(hi, onehot, preferred_element_type=F32).astype(BF16)
    lo = jnp.dot(lo, onehot, preferred_element_type=F32).astype(BF16)
    later = slice(tgt, width - WB)
    for level in range(LEVELS):
        lanes = slice(R * level, R * level + R)
        copies[2 + level].wait()
        h = mm((hi, lo), halves(v_ref[level])) * scale[level]
        keep_ref[:half, lanes] = jnp.where(core == 0, h[:half], h[half:tgt])
        give_ref[:half, lanes] = jnp.where(core == 0, h[half:tgt], h[:half])
        keep_ref[half:, lanes] = h[later]
        give_ref[half:, lanes] = h[later]
        w0_ref[:, :, lanes] = jnp.broadcast_to(h[width - WB :][None], (w0_ref.shape[0], WB, R))
    out.wait()


def leaf_sum_kernel(parts_ref, out_ref):
    total = (parts_ref[0] + parts_ref[1]) + (parts_ref[2] + parts_ref[3])
    out_ref[...] = jnp.broadcast_to(total[None], out_ref.shape)


def block(ref, side, rows, lanes):
    part = ref[side, :, rows, lanes]
    return part.reshape(GROUPS * WB, part.shape[-1])


def couple(g_ref, side, lanes):
    rows = g_ref.shape[2]
    return block(g_ref, side, slice(rows - WB, rows), lanes)


def inverse_kernel(side_ref, g_ref, inv_ref):
    own = side_ref[0]
    inv_ref[...] = pair_inverse(couple(g_ref, own, slice(0, R)), couple(g_ref, 1 - own, slice(0, R)))


def last_inverse_kernel(own_ref, sib_ref, inv_ref):
    inv_ref[...] = pair_inverse(own_ref[...], sib_ref[...])


def advance(top_own, top_sib, low_own, low_sib, inv):
    a_own, a_sib = halves(top_own[:, :R]), halves(top_sib[:, :R])
    c, c_own, c_sib = coefficients(low_own[:, :R], low_sib[:, :R], a_own, a_sib, halves(inv))
    return c, (low_own[:, R:] + low_sib[:, R:]) - (
        mm(c_own, halves(top_own[:, R:])) + mm(c_sib, halves(top_sib[:, R:]))
    )


def basis0_kernel(side_ref, inv_ref, g_ref, w_own_ref, w_sib_ref, w_ref, c_hbm, send_ref, c_ref, sems):
    own, whole = side_ref[0], slice(0, g_ref.shape[3])
    c_ref[...], w = advance(
        couple(g_ref, own, whole), couple(g_ref, 1 - own, whole), w_own_ref[...], w_sib_ref[...], inv_ref[...]
    )
    out = pltpu.make_async_copy(c_ref, c_hbm, sems.at[0])
    out.start()
    left = w_ref.shape[0]
    w_ref[...] = w[:left]
    send_ref[...] = jnp.broadcast_to(w[left:][None], send_ref.shape)
    out.wait()


def basis1_kernel(side_ref, inv_ref, g_ref, w_own_ref, w_sib_ref, c0_hbm, c_ref, send_ref, c0_ref, sems):
    earlier = pltpu.make_async_copy(c0_hbm, c0_ref, sems.at[0])
    earlier.start()
    own, whole = side_ref[0], slice(0, g_ref.shape[3])
    c, w = advance(
        couple(g_ref, own, whole), couple(g_ref, 1 - own, whole), w_own_ref[...], w_sib_ref[...], inv_ref[...]
    )
    send_ref[...] = jnp.broadcast_to(w[None], send_ref.shape)
    earlier.wait()
    first = c0_ref.shape[0]
    c_ref[:, :first, :] = jnp.broadcast_to(c0_ref[...][None], (GROUPS, first, R))
    c_ref[:, first:, :] = jnp.broadcast_to(c[None], (GROUPS, *c.shape))


def last_basis_kernel(side_ref, inv_ref, g_ref, a_ref, c_hbm, c_ref, sems):
    own, whole, first = side_ref[0], slice(0, g_ref.shape[3]), slice(0, WB)
    c_ref[...], a_ref[...] = advance(
        couple(g_ref, own, whole),
        couple(g_ref, 1 - own, whole),
        block(g_ref, own, first, whole),
        block(g_ref, 1 - own, first, whole),
        inv_ref[...],
    )
    out = pltpu.make_async_copy(c_ref, c_hbm, sems.at[0])
    out.start()
    out.wait()


def targets_kernel(side_ref, inv_ref, g_ref, t_own_ref, t_sib_ref, t_ref, c_hbm, c_ref, sems):
    own, whole = side_ref[0], slice(0, g_ref.shape[3])
    c_ref[...], t = advance(
        couple(g_ref, own, whole), couple(g_ref, 1 - own, whole), t_own_ref[...], t_sib_ref[...], inv_ref[...]
    )
    out = pltpu.make_async_copy(c_ref, c_hbm, sems.at[0])
    out.start()
    t_ref[...] = t
    out.wait()


def pair_kernel(own_ref, up_ref, down_ref, up_pair_ref, down_pair_ref):
    share = own_ref.shape[0]
    for pair_ref, next_ref in ((up_pair_ref, up_ref), (down_pair_ref, down_ref)):
        pair_ref[:share] = own_ref[...]
        pair_ref[share:] = next_ref[...]


def split_sum_kernel(q_ref, moved_ref, t_ref, w_ref):
    half = t_ref.shape[0]
    t_ref[...] = q_ref[:half] + moved_ref[:half]
    w_ref[...] = q_ref[half:] + moved_ref[half:]


def total_kernel(inv_ref, a_own_ref, a_sib_ref, t_own_ref, t_sib_ref, *refs):
    far, (cw_ref, k_ref), near, sems = refs[:4], refs[4:6], refs[6:10], refs[10]
    copies = [pltpu.make_async_copy(a, b, sems.at[i]) for i, (a, b) in enumerate(zip(far, near))]
    for copy in copies:
        copy.start()
    t0_ref, t1_ref, t2_ref, w2_ref = near
    k3, k3h, _ = coefficients(
        t_own_ref[...], t_sib_ref[...], halves(a_own_ref[...]), halves(a_sib_ref[...]), halves(inv_ref[...])
    )
    for copy in copies:
        copy.wait()
    w = lambda i: halves(cw_ref[:, i * WB : i * WB + WB, :].reshape(GROUPS * WB, R))
    k2 = t2_ref[...] - mm(k3h, halves(w2_ref[...]))
    k2h = halves(k2)
    k1 = t1_ref[...] - (mm(k2h, w(4)) + mm(k3h, w(3)))
    k1h = halves(k1)
    k0 = t0_ref[...] - (mm(k1h, w(2)) + mm(k2h, w(1)) + mm(k3h, w(0)))
    for level, k in enumerate((k0, k1, k2, k3)):
        k_ref[:, R * level : R * level + R] = k


def final_kernel(core_ref, col_ref, xt_ref, wt_ref, *refs):
    part_refs, (k_own_ref, k_sib_ref, out_hbm, w_ref, out_ref, near_ref, sems) = refs[:5], refs[5:]
    near = pltpu.make_async_copy(xt_ref, near_ref, sems.at[1])
    near.start()
    tgt, rows = out_ref.shape
    core, col = core_ref[0], col_ref[0]
    w_ref[col] = wt_ref[...]
    share = wt_ref.shape[0]
    for shifts, part_ref in zip(((1,), (-1,), (2, 3), (-2, -3), (4,)), part_refs):
        for i, shift in enumerate(shifts):
            w_ref[lax.rem(col + (shift + GROUPS), GROUPS)] = part_ref[i * share : i * share + share]
    own, sib = k_own_ref[...], k_sib_ref[...]
    k = halves(jnp.concatenate([jnp.where(core == 0, own, sib), jnp.where(core == 0, sib, own)], axis=0))
    at = [(LEVELS - 1 - level) * WB for level in range(LEVELS)]
    w = halves(jnp.concatenate([w_ref[:, a : a + WB, :].reshape(GROUPS * WB, rows) for a in at], axis=0))
    half = tgt // 2
    outs = []
    for i in range(2):
        part = slice(i * half, i * half + half)
        total = mm((k[0][part], k[1][part]), w)
        if i == 0:
            near.wait()
        out_ref[part] = near_ref[part] - total
        outs.append(pltpu.make_async_copy(out_ref.at[part], out_hbm.at[part], sems.at[2 * i]))
        outs[-1].start()
    for out in outs:
        out.wait()


def call(kernel, outs, scalars=0, scratch=(), far=(), from_hbm=(), limit=16):
    shapes = [pltpu.HBM(s, F32) if i in far else pltpu.VMEM(s, F32) for i, s in enumerate(outs)]
    single = len(shapes) == 1
    vmem, smem = pl.BlockSpec(memory_space=pltpu.VMEM), pl.BlockSpec(memory_space=pltpu.SMEM)
    hbm = pl.BlockSpec(memory_space=pltpu.HBM)

    def run(*args):
        spaces = [None if i < scalars else pltpu.HBM if i in from_hbm else pltpu.VMEM for i in range(len(args))]
        specs = [smem if m is None else hbm if m is pltpu.HBM else vmem for m in spaces]
        through = [outs[i] for i in far] + [args[i].shape for i in from_hbm]
        return pl.pallas_call(
            kernel,
            out_shape=shapes[0] if single else shapes,
            in_specs=specs,
            out_specs=(hbm if far else vmem) if single else [hbm if i in far else vmem for i in range(len(outs))],
            scratch_shapes=[pltpu.VMEM(shape, F32) for shape in (*scratch, *through)]
            + ([pltpu.SemaphoreType.DMA((len(through) + 1,))] if through else []),
            compiler_params=pltpu.CompilerParams(vmem_limit_bytes=limit * 2**20),
        )(*(a if m is None else pltpu.with_memory_space_constraint(a, m) for a, m in zip(args, spaces)))

    return run


def swap(v, axis):
    return lax.ppermute(v, axis, [(0, 1), (1, 0)])


def mirror(v, axes):
    n = lax.axis_size(axes)
    return lax.ppermute(v, axes, [(i, n - 1 - i) for i in range(n)])


def exchange(v, axes):
    return lax.all_to_all(v, axes, 0, 0, tiled=True).reshape(2, GROUPS, *v.shape[1:])


def mirror_exchange(v, axes):
    n = lax.axis_size(axes)
    pairs = [[p * GROUPS + y for p in (a, n - 1 - a) for y in range(GROUPS)] for a in range(n // 2)]
    out = lax.all_to_all(v, (*axes, "cols"), 0, 0, tiled=True, axis_index_groups=pairs)
    return out.reshape(2, GROUPS, *v.shape[1:])


Z, X = ("z4", "z2", "z1"), ("x2", "x1")


def sweep(columns, row_bases, order):
    rows, width = columns.shape
    tgt = width - LEVELS * WB
    half = tgt // 2
    wide = LEVELS * R
    scale = [0.55 / math.sqrt(R * rows * (4 << level)) for level in range(LEVELS)]
    index = lambda axis: lax.axis_index(axis).astype(jnp.int32)[None]
    core = index("core")
    sides = [index(axis) for axis in ("z2", "z4", "x1")]

    def project(core_ref, order_hbm, x_hbm, v_hbm, *refs):
        project_kernel(core_ref, order_hbm, x_hbm, v_hbm, scale, *refs)

    early = half + (LEVELS - 1) * WB
    hbm, vmem = pl.BlockSpec(memory_space=pltpu.HBM), pl.BlockSpec(memory_space=pltpu.VMEM)
    xt, wt, w0, keep, give = pl.pallas_call(
        project,
        out_shape=[pltpu.HBM((tgt, rows), F32)]
        + [pltpu.VMEM(s, F32) for s in ((LEVELS * WB, rows), (4, WB, wide), (early, wide), (early, wide))],
        in_specs=[pl.BlockSpec(memory_space=pltpu.SMEM), hbm, hbm, hbm],
        out_specs=[hbm] + [vmem] * 4,
        scratch_shapes=[
            pltpu.VMEM(order.shape, jnp.int32),
            pltpu.VMEM(columns.shape, F32),
            pltpu.VMEM(row_bases.shape, F32),
            pltpu.VMEM((tgt, rows), F32),
            pltpu.SemaphoreType.DMA((3 + LEVELS,)),
        ],
        name="project",
        compiler_params=pltpu.CompilerParams(vmem_limit_bytes=40 * 2**20),
    )(core, *(pltpu.with_memory_space_constraint(v, pltpu.HBM) for v in (order, columns, row_bases)))

    q = keep + swap(give, "core")
    w0 = lax.all_to_all(lax.optimization_barrier((w0, q))[0], ("z1", "core"), 0, 0, tiled=True)
    moved = swap(q, "z1")
    t, w = call(split_sum_kernel, [(half, wide), (early - half, wide)])(q, moved)
    send = call(leaf_sum_kernel, [(2 * GROUPS, WB, wide)])(w0)
    g0 = exchange(send, ("z2", "cols"))
    w_sib = swap(w, "z2")
    t_sib = swap(t, "z2")

    def ring(v, shift):
        return lax.ppermute(v, "cols", [((y + shift) % GROUPS, y) for y in range(GROUPS)])

    up, down = ring(wt, 1), ring(wt, -1)
    share = LEVELS * WB
    pairs = call(pair_kernel, [(2 * share, rows), (2 * share, rows)])(wt, up, down)
    up2, down2 = ring(pairs[0], 2), ring(pairs[1], -2)
    parts = (up, down, up2, down2, ring(up2[share:], 1))

    inv0 = call(inverse_kernel, [(R, R)], 1)(sides[0], g0)
    w, cw0, send = call(
        basis0_kernel, [(2 * WB, 3 * R), (3 * WB, R), (2 * GROUPS, WB, 3 * R)], 1, far=(1,)
    )(sides[0], inv0, g0, w, w_sib)
    g1 = mirror_exchange(send, Z)
    w_sib = mirror(w, Z)
    t, t0 = call(targets_kernel, [(half, 3 * R), (half, R)], 1, far=(1,))(sides[0], inv0, g0, t, t_sib)
    t_sib = mirror(t, Z)

    inv1 = call(inverse_kernel, [(R, R)], 1)(sides[1], g1)
    cw, send = call(
        basis1_kernel, [(GROUPS, 5 * WB, R), (2 * GROUPS, 2 * WB, 2 * R)], 1, from_hbm=(5,)
    )(sides[1], inv1, g1, w, w_sib, cw0)
    g2 = exchange(send, ("x1", "cols"))
    t, t1 = call(targets_kernel, [(half, 2 * R), (half, R)], 1, far=(1,))(sides[1], inv1, g1, t, t_sib)
    t_sib = swap(t, "x1")

    inv2 = call(inverse_kernel, [(R, R)], 1)(sides[2], g2)
    a3, cw2 = call(last_basis_kernel, [(R, R), (R, R)], 1, far=(1,))(sides[2], inv2, g2)
    a3_sib = mirror(a3, X)
    cw = lax.all_to_all(cw, "cols", 0, 0, tiled=True)
    t, t2 = call(targets_kernel, [(half, R), (half, R)], 1, far=(1,))(sides[2], inv2, g2, t, t_sib)
    t_sib = mirror(t, X)

    inv3 = call(last_inverse_kernel, [(R, R)])(a3, a3_sib)
    k = call(total_kernel, [(half, wide)], from_hbm=(5, 6, 7, 8))(inv3, a3, a3_sib, t, t_sib, t0, t1, t2, cw2, cw)
    k_sib = swap(k, "core")
    return call(final_kernel, [(tgt, rows)], 2, [(GROUPS, LEVELS * WB, rows)], (0,), (2,), 24)(
        core, index("cols"), xt, wt, *parts, k, k_sib
    ).T


def solution(mesh):
    fine = Mesh(mesh.devices.reshape(2, 2, 2, 2, 2, 2, GROUPS), (*ROW_AXES, "cols"))
    placed = (P(ROW_AXES, "cols"), P(None, ROW_AXES, None), P(ROW_AXES, None))
    return jax.shard_map(sweep, mesh=fine, in_specs=placed, out_specs=P(ROW_AXES, "cols"), check_vma=False)
```
